32 devices in a mesh: sec: 2 (over x), gx: 4 (over y, core), gz: 4 (over z).
Axes of the slice: x: 2, y: 2, z: 4, core: 2. Of those that a mesh axis runs over, the one named last changes fastest.
Arguments:
- velocity: float32 [2, 3, 128, 32, 512], P('sec', None, 'gx', 'gz'), may hold values from -6 to 6
- drag: float32 [2, 128, 32, 512], P('sec', 'gx', 'gz'), may hold values from 0.2 to 2
- stream_gain: float32 [65], replicated, may hold values from 0.5 to 2
- span_gain: float32 [257], replicated, may hold values from 0.5 to 2
Outputs:
- advanced: float32 [2, 3, 128, 32, 512], P('sec', None, 'gx', 'gz')
The draws below stay inside these ranges and needn't reach their ends.
All inputs are finite; a program needn't handle non-finite values.
Results may differ from the reference program's by a relative error of at most 0.00005.
Values sent between devices are 32-bit elements; how exact they have to be, the bound alone decides.
No kernel may reach another device: no remote copies, remote signals or barrier semaphores. Data moves between devices by JAX's collectives and lax.ppermute only.
A program may use at most 128 MiB of HBM per device.

```python
import math
import jax
import jax.numpy as jnp

NY = 512
NX = 128
NZ = 32


def shard_levels(key, shape, pieces, least, largest):
    factor_of, own = 1.0, jax.random.fold_in(key, 6)
    for axis_at, shards_of in pieces:
        steps = jnp.exp(jax.random.uniform(jax.random.fold_in(own, axis_at), (shards_of,), jnp.float32, least / len(pieces), largest / len(pieces)))
        factor_of = factor_of * jnp.repeat(steps, shape[axis_at] // shards_of).reshape([-1 if axis == axis_at else 1 for axis in range(len(shape))])
    return factor_of


def gaussian(stream_key, shape, spread, most, shards=(), kind=jnp.bfloat16):
    values = jax.random.normal(stream_key, shape, jnp.float32) * spread
    if len(shards) > 0:
        values = shard_levels(stream_key, shape, shards, -0.22, 0.18) * values
    return jnp.clip(values, min=-most, max=most).astype(kind)


def setup_inputs(seed: int = 0) -> dict:
    streams_of = jax.random.split(jax.random.key(seed), 5)
    velocity = gaussian(streams_of[0], (2, 3, NX, NZ, NY), 1.0, 6.0, ((0, 2), (2, 4), (3, 4)), jnp.float32)
    drag = jnp.clip(jnp.exp(math.log(2.0) - 2.3025851 * jax.random.uniform(streams_of[1], (2, NX, NZ, NY), jnp.float32) ** shard_levels(streams_of[1], (2, NX, NZ, NY), ((0, 2), (1, 4), (2, 4)), -0.2, 0.2)), 0.2, 2.0)
    stream_gain = jnp.clip(jnp.exp(jax.random.uniform(streams_of[2], (NX // 2 + 1,), jnp.float32, math.log(0.5), math.log(2.0))), 0.5, 2.0)
    span_gain = jnp.clip(jnp.exp(jax.random.uniform(streams_of[3], (NY // 2 + 1,), jnp.float32, math.log(0.5), math.log(2.0))), 0.5, 2.0)
    return dict(velocity=velocity, drag=drag, stream_gain=stream_gain, span_gain=span_gain)


fringe_peak = 4.0
time_step = 0.05


def spectral(signal, along, gains):
    length = signal.shape[along]
    modes = jnp.arange(length // 2 + 1)
    wavenum = jnp.where(modes == length // 2, 0.0, 2.0 * jnp.pi * modes / length) * gains
    dims_shape = [1] * signal.ndim
    dims_shape[along] = length // 2 + 1
    spectrum = jnp.fft.rfft(signal, axis=along)
    result = jnp.fft.irfft(1j * wavenum.reshape(dims_shape) * spectrum, n=length, axis=along)
    return result.astype(signal.dtype)


def tendency(fields, drag, stream_gain, span_gain):
    grad_x = spectral(fields, 2, stream_gain)
    grad_y = spectral(fields, 4, span_gain)
    padded = jnp.pad(fields, ((0, 0), (0, 0), (0, 0), (1, 1), (0, 0)))
    grad_z = 0.5 * (padded[:, :, :, 2:] - padded[:, :, :, :-2])
    advect = fields[:, 0:1] * grad_x + fields[:, 1:2] * grad_y + fields[:, 2:3] * grad_z
    cells = jnp.arange(NX)
    fringe_start = 3 * NX // 4
    fringe_width = NX // 4
    phases = (cells - fringe_start).astype(jnp.float32) + 0.5
    profile = jnp.where(cells >= fringe_start, fringe_peak * jnp.sin(jnp.pi * phases / fringe_width) ** 2, 0.0)
    relax = profile[None, :, None, None] * (fields[0] - fields[1])
    forcing = jnp.stack([jnp.zeros_like(relax), relax])
    resist = -drag[:, None] * jnp.abs(fields[:, 0:1]) * fields
    return -advect + resist + forcing


def reference(velocity, drag, stream_gain, span_gain):
    first = velocity + time_step * tendency(velocity, drag, stream_gain, span_gain)
    return 0.5 * velocity + 0.5 * (first + time_step * tendency(first, drag, stream_gain, span_gain))
```

```python
import functools

import jax
import jax.numpy as jnp
import numpy as np
from jax import lax
from jax.experimental import pallas as pl
from jax.experimental.pallas import tpu as pltpu
from jax.sharding import PartitionSpec as P

fringe_peak = 4.0
time_step = 0.05
lanes = 128
f32 = jnp.float32
bf16 = jnp.bfloat16


def extended(cells, sides, width):
    for axis, dim in sides:
        count = lax.axis_size(axis)
        ends = count - 1
        head = lax.slice_in_dim(cells, 0, width, axis=dim)
        tail = lax.slice_in_dim(cells, cells.shape[dim] - width, cells.shape[dim], axis=dim)
        cells = jnp.concatenate(
            [
                lax.ppermute(tail, axis, [(i, (i + 1) % count) for i in range(ends)]),
                cells,
                lax.ppermute(head, axis, [((i + 1) % count, i) for i in range(ends)]),
            ],
            axis=dim,
        )
    return cells


def from_behind(x, axis, by):
    peers = lax.axis_size(axis)
    pairs = [(i, i + by) for i in range(peers) if 0 <= i + by < peers]
    return lax.ppermute(x, axis, pairs)


def kernel_table(gains, length):
    half = length // 2
    shifts = lax.broadcasted_iota(jnp.int32, (length, half), 0)
    modes = lax.broadcasted_iota(jnp.int32, (length, half), 1)
    phases = (shifts * modes % length).astype(jnp.float32) * (2.0 * jnp.pi / length)
    wavenum = jnp.arange(half, dtype=jnp.float32) * (2.0 * jnp.pi / length)
    weights = gains[:half] * wavenum
    kernel = -(2.0 / length) * jnp.dot(jnp.sin(phases), weights, precision=lax.Precision.HIGHEST)
    flipped = jnp.concatenate([kernel[:1], kernel[1:][::-1]])
    leading = jnp.tile(flipped, length)[: length * (length - 1)].reshape(length, length - 1)
    return jnp.concatenate([leading, flipped[::-1][:, None]], axis=1)


def fringe_profile(anchor, number, total):
    cells = anchor + jnp.arange(number, dtype=jnp.int32)
    fringe_start = 3 * total // 4
    fringe_width = total // 4
    phases = (cells - fringe_start).astype(jnp.float32) + 0.5
    return jnp.where(
        cells >= fringe_start, fringe_peak * jnp.sin(jnp.pi * phases / fringe_width) ** 2, 0.0
    )


def general_step(velocity, drag, stream_gain, span_gain):
    start_fields = velocity[0]
    drag_here = drag[0]
    cells_x = start_fields.shape[1]
    width_y = start_fields.shape[3]
    groups = lax.axis_size("gx")
    total_x = cells_x * groups
    table_x = kernel_table(stream_gain, total_x)
    table_y = kernel_table(span_gain, width_y)
    is_farm = (lax.axis_index("sec") == 1).astype(jnp.float32)

    def tendency(fields):
        block_shape = fields.shape
        flat_block = fields.reshape(3, cells_x, -1)
        pencils = lax.all_to_all(flat_block, "gx", split_axis=2, concat_axis=1, tiled=True)
        gradient = jnp.stack(
            [jnp.dot(table_x, pencils[comp], precision=lax.Precision.HIGHEST) for comp in range(3)]
        )
        returned = lax.all_to_all(gradient, "gx", split_axis=1, concat_axis=2, tiled=True).reshape(
            block_shape
        )
        grad_y = jnp.dot(
            fields.reshape(-1, width_y), table_y.T, precision=lax.Precision.HIGHEST
        ).reshape(block_shape)
        padded = extended(fields, (("gz", 2),), 1)
        grad_z = 0.5 * (padded[:, :, 2:] - padded[:, :, :-2])
        resist = -drag_here[None] * jnp.abs(fields[0:1]) * fields
        upstream = from_behind(fields, "sec", 1)
        profile = fringe_profile(lax.axis_index("gx") * cells_x, cells_x, total_x)
        relax = is_farm * profile[None, :, None, None] * (upstream - fields)
        advect = fields[0:1] * returned + fields[1:2] * grad_y + fields[2:3] * grad_z
        return -advect + resist + relax

    first = start_fields + time_step * tendency(start_fields)
    advanced = 0.5 * start_fields + 0.5 * (first + time_step * tendency(first))
    return advanced[None]


def level_of(q, side):
    return 2 * q + (side if q % 2 == 0 else 1 - side)


def pack_kernel(G, X, L, v_ref, d_ref, o_ref):
    odd = lax.axis_index("gz") % 2
    for q in range(G):
        slot = jnp.where(odd == 1, G - 1 - q, q)
        for side in range(2):
            lev = level_of(q, side)
            for c in range(3):
                o_ref[slot, side, c] = v_ref[pl.ds(c * X * L + lev, X, stride=L), :]
            o_ref[slot, side, 3] = d_ref[pl.ds(lev, X, stride=L), :]


def unpack_kernel(G, X, L, r_ref, o_ref):
    odd = lax.axis_index("gz") % 2
    for q in range(G):
        slot = jnp.where(odd == 1, G - 1 - q, q)
        for side in range(2):
            lev = level_of(q, side)
            for c in range(3):
                o_ref[pl.ds(c * X * L + lev, X, stride=L), :] = r_ref[slot, side, c]


def bases(length):
    half = length // 2
    at = np.outer(np.arange(length), np.arange(half)) % length * (2.0 * np.pi / length)
    sin, cos = np.sin(at), np.cos(at)
    left = np.concatenate([sin, -cos], axis=1)
    right = np.concatenate([cos, sin], axis=1)
    scale = -(2.0 / length) * np.arange(half) * (2.0 * np.pi / length)
    return (
        jnp.asarray(left, f32),
        jnp.asarray(right, f32),
        jnp.asarray(np.concatenate([scale, scale])[None], f32),
    )


def split(x):
    high = x.astype(bf16)
    return high, (x - high.astype(f32)).astype(bf16)


def table_kernel(lx, rx, gx, ly, ry, gy, tx_ref, ty_ref):
    def table(left, right, gain):
        return lax.dot_general(
            left[...] * gain[...],
            right[...],
            (((1,), (1,)), ((), ())),
            precision=lax.Precision.HIGHEST,
            preferred_element_type=f32,
        )

    high, low = split(table(lx, rx, gx))
    tx_ref[0], tx_ref[1] = high, low
    high, low = split(-table(ly, ry, gy))
    ty_ref[0], ty_ref[1] = high, low


def slope_kernel(r_ref, tx_ref, ty_ref, o_ref):
    G, _, _, X, Y = r_ref.shape
    full = [r_ref[:, 0, c].reshape(G * X, Y) for c in range(3)]
    txh, txl = tx_ref[0], tx_ref[1]
    tyh, tyl = ty_ref[0], ty_ref[1]
    dot = functools.partial(jnp.dot, preferred_element_type=f32)
    for c in range(3):
        high, low = split(full[c])
        dx = dot(txh, high) + (dot(txl, high) + dot(txh, low))
        dy = dot(high, tyh) + (dot(high, tyl) + dot(low, tyh))
        o_ref[:, 0, c] = (full[0] * dx + full[1] * dy).reshape(G, X, Y)


def evaluate(w, slope, out_halo, in_halo, upstream, lam, sign, drag):
    result = []
    for side in range(2):
        u, _, h = w[side]
        push = drag[side] * jnp.abs(u)
        rows = []
        for c in range(3):
            here = w[side][c]
            if side == 0:
                dz = sign * (w[1][c] - out_halo[c])
            else:
                dz = sign * (in_halo[c] - w[0][c])
            rows.append(
                lam * (upstream[side][c] - here) - (slope[side][c] + h * dz) - push * here
            )
        result.append(rows)
    return result


def half_sign():
    odd = (lax.axis_index("gx") + lax.axis_index("gz")) % 2
    return jnp.where(odd == 1, -0.5, 0.5).astype(f32)


def point_kernel(fringe, last, *refs):
    if last:
        r_ref, w_ref, s_ref, a_ref, b_ref, u_ref, l_ref, o_ref = refs
    else:
        r_ref, s_ref, a_ref, b_ref, u_ref, l_ref, o_ref = refs
        w_ref = r_ref
    both = range(2)
    three = range(3)
    k = pl.program_id(0)
    lam = jnp.where(k >= fringe, l_ref[0], 0.0)
    w = [[w_ref[0, s, c] for c in three] for s in both]
    rate = evaluate(
        w,
        [[s_ref[0, s, c] for c in three] for s in both],
        [a_ref[0, c] for c in three],
        [b_ref[0, c] for c in three],
        [[u_ref[0, s, c] for c in three] for s in both],
        lam,
        half_sign(),
        [r_ref[0, s, 3] for s in both],
    )
    for s in both:
        for c in three:
            moved = w[s][c] + time_step * rate[s][c]
            o_ref[0, s, c] = 0.5 * r_ref[0, s, c] + 0.5 * moved if last else moved


def transposed_step(velocity, drag, stream_gain, span_gain):
    _, _, X, L, Y = velocity.shape
    G, Z = lax.axis_size("gx"), lax.axis_size("gz")
    total = X * G
    fringe = 3 * G // 4
    wide = G - fringe

    def place(gz, q):
        return (q if gz % 2 == 0 else G - 1 - q) * Z + gz

    inner, outer = [], []
    for gz in range(Z):
        for q in range(G - 1):
            pair = (place(gz, q), place(gz, q + 1))
            (inner if q % 2 == 0 else outer).extend([pair, pair[::-1]])
        if gz + 1 < Z:
            pair = (place(gz, G - 1), place(gz + 1, 0))
            outer.extend([pair, pair[::-1]])

    packed = pl.pallas_call(
        functools.partial(pack_kernel, G, X, L),
        grid=(Y // lanes,),
        in_specs=[
            pl.BlockSpec((3 * X * L, lanes), lambda i: (0, i)),
            pl.BlockSpec((X * L, lanes), lambda i: (0, i)),
        ],
        out_specs=pl.BlockSpec((G, 2, 4, X, lanes), lambda i: (0, 0, 0, 0, i)),
        out_shape=jax.ShapeDtypeStruct((G, 2, 4, X, Y), f32),
        name="pack",
    )(velocity.reshape(3 * X * L, Y), drag.reshape(X * L, Y))
    rows = lax.all_to_all(packed, "gx", 0, 0, tiled=True)

    lx, rx, sx = bases(total)
    ly, ry, sy = bases(Y)
    gx = jnp.concatenate([stream_gain[: total // 2]] * 2)[None] * sx
    gy = jnp.concatenate([span_gain[: Y // 2]] * 2)[None] * sy
    tx, ty = pl.pallas_call(
        table_kernel,
        out_shape=(
            jax.ShapeDtypeStruct((2, total, total), bf16),
            jax.ShapeDtypeStruct((2, Y, Y), bf16),
        ),
        cost_estimate=pl.CostEstimate(
            flops=12 * Y * Y * Y, bytes_accessed=12 * Y * Y, transcendentals=0
        ),
        name="tables",
    )(lx, rx, gx, ly, ry, gy)

    at = np.arange(wide * X) + 0.5
    profile = fringe_peak * np.sin(np.pi * at / (wide * X)) ** 2
    profile = jnp.broadcast_to(jnp.asarray(profile, f32).reshape(wide, X, 1), (wide, X, Y))
    lam = profile * (lax.axis_index("sec") == 1).astype(f32)

    def halos(w):
        facing_out = lax.ppermute(w[:, 0, :3], ("gx", "gz"), outer)
        facing_in = lax.ppermute(w[:, 1, :3], ("gx", "gz"), inner)
        upstream = lax.ppermute(w[fringe:, :, :3], "sec", [(0, 1)])
        return facing_out, facing_in, upstream

    def slopes(w):
        n = w.shape[2]
        return pl.pallas_call(
            slope_kernel,
            grid=(2,),
            in_specs=[
                pl.BlockSpec((G, 1, n, X, Y), lambda s: (0, s, 0, 0, 0)),
                pl.BlockSpec((2, total, total), lambda s: (0, 0, 0)),
                pl.BlockSpec((2, Y, Y), lambda s: (0, 0, 0)),
            ],
            out_specs=pl.BlockSpec((G, 1, 3, X, Y), lambda s: (0, s, 0, 0, 0)),
            out_shape=jax.ShapeDtypeStruct((G, 2, 3, X, Y), f32),
            cost_estimate=pl.CostEstimate(
                flops=36 * total * Y * (total + Y), bytes_accessed=56 * total * Y, transcendentals=0
            ),
            name="slopes",
        )(w, tx, ty)

    def points(last, *operands):
        def block(k):
            return (k, 0, 0, 0, 0)

        def plane(k):
            return (k, 0, 0, 0)

        def late(k):
            return (jnp.maximum(k - fringe, 0), 0, 0, 0, 0)

        fields = [pl.BlockSpec((1, 2, 4, X, Y), block)]
        if last:
            fields.append(pl.BlockSpec((1, 2, 3, X, Y), block))
        return pl.pallas_call(
            functools.partial(point_kernel, fringe, last),
            grid=(G,),
            in_specs=fields
            + [
                pl.BlockSpec((1, 2, 3, X, Y), block),
                pl.BlockSpec((1, 3, X, Y), plane),
                pl.BlockSpec((1, 3, X, Y), plane),
                pl.BlockSpec((1, 2, 3, X, Y), late),
                pl.BlockSpec((1, X, Y), lambda k: (jnp.maximum(k - fringe, 0), 0, 0)),
            ],
            out_specs=pl.BlockSpec((1, 2, 3, X, Y), block),
            out_shape=jax.ShapeDtypeStruct((G, 2, 3, X, Y), f32),
            cost_estimate=pl.CostEstimate(
                flops=100 * total * Y, bytes_accessed=120 * total * Y, transcendentals=0
            ),
            name="points",
        )(*operands)

    first = points(False, rows, slopes(rows), *halos(rows), lam)
    result = points(True, rows, first, slopes(first), *halos(first), lam)
    back = lax.all_to_all(result, "gx", 0, 0, tiled=True)
    advanced = pl.pallas_call(
        functools.partial(unpack_kernel, G, X, L),
        grid=(Y // lanes,),
        in_specs=[pl.BlockSpec((G, 2, 3, X, lanes), lambda i: (0, 0, 0, 0, i))],
        out_specs=pl.BlockSpec((3 * X * L, lanes), lambda i: (0, i)),
        out_shape=jax.ShapeDtypeStruct((3 * X * L, Y), f32),
        name="unpack",
    )(back)
    return advanced.reshape(velocity.shape)


def shards(velocity, drag, stream_gain, span_gain):
    groups = lax.axis_size("gx")
    levels, width = velocity.shape[3:]
    form = transposed_step if groups % 4 == 0 and levels == 2 * groups and width % lanes == 0 else general_step
    return form(velocity, drag, stream_gain, span_gain)


def solution(mesh):
    placed = (P("sec", None, "gx", "gz", None), P("sec", "gx", "gz", None), P(), P())
    return jax.shard_map(
        shards,
        mesh=mesh,
        in_specs=placed,
        out_specs=P("sec", None, "gx", "gz", None),
        check_vma=False,
    )
```

```python
import functools

import jax
import jax.numpy as jnp
import numpy as np
from jax import lax
from jax.experimental import pallas as pl
from jax.experimental.pallas import tpu as pltpu
from jax.sharding import PartitionSpec as P

fringe_peak = 4.0
time_step = 0.05
lanes = 128
f32 = jnp.float32
bf16 = jnp.bfloat16


def extended(cells, sides, width):
    for axis, dim in sides:
        count = lax.axis_size(axis)
        ends = count - 1
        head = lax.slice_in_dim(cells, 0, width, axis=dim)
        tail = lax.slice_in_dim(cells, cells.shape[dim] - width, cells.shape[dim], axis=dim)
        cells = jnp.concatenate(
            [
                lax.ppermute(tail, axis, [(i, (i + 1) % count) for i in range(ends)]),
                cells,
                lax.ppermute(head, axis, [((i + 1) % count, i) for i in range(ends)]),
            ],
            axis=dim,
        )
    return cells


def from_behind(x, axis, by):
    peers = lax.axis_size(axis)
    pairs = [(i, i + by) for i in range(peers) if 0 <= i + by < peers]
    return lax.ppermute(x, axis, pairs)


def kernel_table(gains, length):
    half = length // 2
    shifts = lax.broadcasted_iota(jnp.int32, (length, half), 0)
    modes = lax.broadcasted_iota(jnp.int32, (length, half), 1)
    phases = (shifts * modes % length).astype(jnp.float32) * (2.0 * jnp.pi / length)
    wavenum = jnp.arange(half, dtype=jnp.float32) * (2.0 * jnp.pi / length)
    weights = gains[:half] * wavenum
    kernel = -(2.0 / length) * jnp.dot(jnp.sin(phases), weights, precision=lax.Precision.HIGHEST)
    flipped = jnp.concatenate([kernel[:1], kernel[1:][::-1]])
    leading = jnp.tile(flipped, length)[: length * (length - 1)].reshape(length, length - 1)
    return jnp.concatenate([leading, flipped[::-1][:, None]], axis=1)


def fringe_profile(anchor, number, total):
    cells = anchor + jnp.arange(number, dtype=jnp.int32)
    fringe_start = 3 * total // 4
    fringe_width = total // 4
    phases = (cells - fringe_start).astype(jnp.float32) + 0.5
    return jnp.where(
        cells >= fringe_start, fringe_peak * jnp.sin(jnp.pi * phases / fringe_width) ** 2, 0.0
    )


def general_step(velocity, drag, stream_gain, span_gain):
    start_fields = velocity[0]
    drag_here = drag[0]
    cells_x = start_fields.shape[1]
    width_y = start_fields.shape[3]
    groups = lax.axis_size("gx")
    total_x = cells_x * groups
    table_x = kernel_table(stream_gain, total_x)
    table_y = kernel_table(span_gain, width_y)
    is_farm = (lax.axis_index("sec") == 1).astype(jnp.float32)

    def tendency(fields):
        block_shape = fields.shape
        flat_block = fields.reshape(3, cells_x, -1)
        pencils = lax.all_to_all(flat_block, "gx", split_axis=2, concat_axis=1, tiled=True)
        gradient = jnp.stack(
            [jnp.dot(table_x, pencils[comp], precision=lax.Precision.HIGHEST) for comp in range(3)]
        )
        returned = lax.all_to_all(gradient, "gx", split_axis=1, concat_axis=2, tiled=True).reshape(
            block_shape
        )
        grad_y = jnp.dot(
            fields.reshape(-1, width_y), table_y.T, precision=lax.Precision.HIGHEST
        ).reshape(block_shape)
        padded = extended(fields, (("gz", 2),), 1)
        grad_z = 0.5 * (padded[:, :, 2:] - padded[:, :, :-2])
        resist = -drag_here[None] * jnp.abs(fields[0:1]) * fields
        upstream = from_behind(fields, "sec", 1)
        profile = fringe_profile(lax.axis_index("gx") * cells_x, cells_x, total_x)
        relax = is_farm * profile[None, :, None, None] * (upstream - fields)
        advect = fields[0:1] * returned + fields[1:2] * grad_y + fields[2:3] * grad_z
        return -advect + resist + relax

    first = start_fields + time_step * tendency(start_fields)
    advanced = 0.5 * start_fields + 0.5 * (first + time_step * tendency(first))
    return advanced[None]


def own_pair():
    flip = lax.axis_index("gz") % 2
    j = lax.axis_index("gx")
    return j ^ (flip * (lax.axis_size("gx") - 1))


def level_of(q, side):
    return 2 * q + ((q & 1) ^ side)


def pack_kernel(X, L, v_ref, d_ref, *outs):
    q = own_pair()
    i = pl.program_id(0)
    at = pl.ds(pl.multiple_of(i * lanes, lanes), lanes)
    for b in range(4):
        for side in range(2):
            lev = level_of(q ^ b, side)
            for c in range(3):
                outs[b][side, c, :, at] = v_ref[pl.ds(c * X * L + lev, X, stride=L), :]
            outs[4 + b][side, :, at] = d_ref[pl.ds(lev, X, stride=L), :]


def unpack_kernel(X, L, *refs):
    o_ref = refs[-1]
    q = own_pair()
    i = pl.program_id(0)
    at = pl.ds(pl.multiple_of(i * lanes, lanes), lanes)
    for b in range(4):
        for side in range(2):
            lev = level_of(q ^ b, side)
            for c in range(3):
                o_ref[pl.ds(c * X * L + lev, X, stride=L), :] = refs[2 * b + side][c, :, at]


def bases(length):
    half = length // 2
    at = np.outer(np.arange(length), np.arange(half)) % length * (2.0 * np.pi / length)
    sin, cos = np.sin(at), np.cos(at)
    left = np.concatenate([sin, -cos], axis=1)
    right = np.concatenate([cos, sin], axis=1)
    scale = -(2.0 / length) * np.arange(half) * (2.0 * np.pi / length)
    return (
        jnp.asarray(left, f32),
        jnp.asarray(right, f32),
        jnp.asarray(np.concatenate([scale, scale])[None], f32),
    )


def split(x):
    high = x.astype(bf16)
    return high, (x - high.astype(f32)).astype(bf16)


def table_kernel(X, lx, rx, gx, ly, ry, gy, tx_ref, ty_ref):
    j = lax.axis_index("gx")

    def relative(ref):
        parts = [ref[pl.ds(pl.multiple_of((j ^ b) * X, X), X), :] for b in range(4)]
        return jnp.concatenate(parts, axis=0)

    def table(left, right, gain):
        return lax.dot_general(
            left * gain,
            right,
            (((1,), (1,)), ((), ())),
            precision=lax.Precision.HIGHEST,
            preferred_element_type=f32,
        )

    n = tx_ref.shape[1]
    high, low = split(table(relative(lx), relative(rx), gx[...]))
    tx_ref[:n], tx_ref[n:] = high, low
    high, low = split(-table(ly[...], ry[...], gy[...]))
    ty_ref[0], ty_ref[1] = high, low


def gather_kernel(X, *refs):
    parts, (out_ref, in_ref, up_ref) = refs[:4], refs[4:]
    j = lax.axis_index("gx")
    for b in range(4):
        rows = pl.ds(b * X, X)
        out_ref[:, rows] = parts[b][0]
        in_ref[:, rows] = parts[b][1]

        @pl.when((j ^ b) == 3)
        def _():
            up_ref[...] = parts[b][...]


def slope_kernel(out_ref, in_ref, tx_ref, ty_ref, so_ref, si_ref):
    n = out_ref.shape[1]
    tx, tyh, tyl = tx_ref[...], ty_ref[0], ty_ref[1]
    dot = functools.partial(jnp.dot, preferred_element_type=f32)
    for w_ref, s_ref in ((out_ref, so_ref), (in_ref, si_ref)):
        for c in range(3):
            high, low = split(w_ref[c])
            both = dot(tx, high)
            dx = both[:n] + (both[n:] + dot(tx[:n], low))
            stack = dot(jnp.concatenate([high, low], axis=0), tyh)
            dy = stack[:n] + (stack[n:] + dot(high, tyl))
            s_ref[c] = w_ref[0] * dx + w_ref[1] * dy


chunk = 8


def fringe_weight(lam_ref, b, r):
    there = ((lax.axis_index("gx") ^ b) == 3) & (lax.axis_index("sec") == 1)
    return jnp.where(there, lam_ref[pl.ds(r, chunk), :], 0.0)


def rates(X, b, r, w, s, h_out, h_in, up_ref, lam_ref, drag, sides):
    q = own_pair()
    sign = jnp.where((q & 1) == 1, -0.5, 0.5).astype(f32)
    cross = jnp.where(((q + 1) & 2) == 2, 3, 0)
    here = pl.ds(pl.multiple_of(b * X + r, chunk), chunk)
    beside = pl.ds(pl.multiple_of((b ^ 1) * X + r, chunk), chunk)
    beyond = pl.ds(pl.multiple_of((b ^ cross) * X + r, chunk), chunk)
    lam = fringe_weight(lam_ref, b, r)
    found = []
    for side in sides:
        own, other = w[side], w[1 - side]
        u, h = own[0, here], own[2, here]
        push = drag[side] * jnp.abs(u)
        rows = []
        for c in range(3):
            value = own[c, here]
            if side == 0:
                dz = sign * (other[c, here] - h_out[c, beyond])
            else:
                dz = sign * (h_in[c, beside] - other[c, here])
            relax = lam * (up_ref[side, c, pl.ds(r, chunk)] - value)
            rows.append(relax - (s[side][c, here] + h * dz) - push * value)
        found.append(rows)
    return found


def first_kernel(X, *refs):
    w, s = refs[0:2], refs[2:4]
    h_out, h_in, up_ref, lam_ref = refs[4:8]
    drags = refs[8:12]
    f, f_up = refs[12:14], refs[14]
    j = lax.axis_index("gx")
    for b in range(4):

        @pl.loop(0, X // chunk)
        def _(i):
            r = pl.multiple_of(i * chunk, chunk)
            at = pl.ds(r, chunk)
            here = pl.ds(pl.multiple_of(b * X + r, chunk), chunk)
            drag = [drags[b][side, at] for side in range(2)]
            found = rates(X, b, r, w, s, h_out, h_in, up_ref, lam_ref, drag, (0, 1))
            for side in range(2):
                for c in range(3):
                    f[side][c, here] = w[side][c, here] + time_step * found[side][c]

        @pl.when((j ^ b) == 3)
        def _():
            for side in range(2):
                f_up[side] = f[side][:, pl.ds(b * X, X)]


def last_kernel(X, side, *refs):
    v_ref = refs[0]
    w = refs[1:3]
    s_ref, halo_ref, up_ref, lam_ref = refs[3:7]
    drags = refs[7:11]
    outs = refs[11:15]
    for b in range(4):

        @pl.loop(0, X // chunk)
        def _(i):
            r = pl.multiple_of(i * chunk, chunk)
            at = pl.ds(r, chunk)
            here = pl.ds(pl.multiple_of(b * X + r, chunk), chunk)
            drag = {side: drags[b][side, at]}
            found = rates(
                X, b, r, w, {side: s_ref}, halo_ref, halo_ref, up_ref, lam_ref, drag, (side,)
            )[0]
            for c in range(3):
                moved = w[side][c, here] + time_step * found[c]
                outs[b][c, at] = 0.5 * v_ref[c, here] + 0.5 * moved


def kernel_call(body, name, inputs, outputs, flops, **more):
    return pl.pallas_call(
        body,
        out_shape=[pltpu.VMEM(shape, kind) for shape, kind in outputs],
        in_specs=[pl.BlockSpec(memory_space=pltpu.VMEM)] * len(inputs),
        out_specs=[pl.BlockSpec(memory_space=pltpu.VMEM)] * len(outputs),
        compiler_params=pltpu.CompilerParams(vmem_limit_bytes=24 << 20),
        cost_estimate=pl.CostEstimate(flops=flops, bytes_accessed=flops // 50, transcendentals=0),
        name=name,
        **more,
    )(*[pltpu.with_memory_space_constraint(x, pltpu.VMEM) for x in inputs])


def transposed_step(velocity, drag, stream_gain, span_gain):
    _, _, X, L, Y = velocity.shape
    G, Z = lax.axis_size("gx"), lax.axis_size("gz")
    total = X * G

    def place(gz, q):
        return (q if gz % 2 == 0 else G - 1 - q) * Z + gz

    outer = []
    for gz in range(Z):
        pairs = [(place(gz, q), place(gz, q + 1)) for q in range(1, G - 1, 2)]
        if gz + 1 < Z:
            pairs.append((place(gz, G - 1), place(gz + 1, 0)))
        outer.extend(pairs + [pair[::-1] for pair in pairs])

    def swap(x, by):
        return lax.ppermute(x, "gx", [(i, i ^ by) for i in range(G)])

    packed = pl.pallas_call(
        functools.partial(pack_kernel, X, L),
        grid=(Y // lanes,),
        in_specs=[
            pl.BlockSpec((3 * X * L, lanes), lambda i: (0, i)),
            pl.BlockSpec((X * L, lanes), lambda i: (0, i)),
        ],
        out_specs=[pl.BlockSpec(memory_space=pltpu.VMEM)] * 8,
        out_shape=[pltpu.VMEM((2, 3, X, Y), f32)] * 4 + [pltpu.VMEM((2, X, Y), f32)] * 4,
        compiler_params=pltpu.CompilerParams(vmem_limit_bytes=24 << 20),
        name="pack",
    )(velocity.reshape(3 * X * L, Y), drag.reshape(X * L, Y))
    blocks, drags = packed[:4], packed[4:]
    blocks = [blocks[0]] + [swap(blocks[b], b) for b in range(1, 4)]
    drags = [drags[0]] + [swap(drags[b], b) for b in range(1, 4)]

    lx, rx, sx = bases(total)
    ly, ry, sy = bases(Y)
    gx = jnp.concatenate([stream_gain[: total // 2]] * 2)[None] * sx
    gy = jnp.concatenate([span_gain[: Y // 2]] * 2)[None] * sy
    tx, ty = kernel_call(
        functools.partial(table_kernel, X),
        "tables",
        (lx, rx, gx, ly, ry, gy),
        (((2 * total, total), bf16), ((2, Y, Y), bf16)),
        12 * Y * Y * Y,
    )

    at = np.arange(X) + 0.5
    profile = fringe_peak * np.sin(np.pi * at / X) ** 2
    lam = jnp.broadcast_to(jnp.asarray(profile, f32)[:, None], (X, Y))
    plane = ((3, total, Y), f32)
    fringe = ((2, 3, X, Y), f32)

    def exchange(planes, up):
        return (
            lax.ppermute(up, "sec", [(0, 1)]),
            lax.ppermute(planes[0], ("gx", "gz"), outer),
            swap(planes[1], 1),
        )

    def slopes(planes):
        return kernel_call(
            slope_kernel,
            "slopes",
            (*planes, tx, ty),
            (plane, plane),
            36 * total * Y * (total + Y),
        )

    *start, up = kernel_call(
        functools.partial(gather_kernel, X), "gather", blocks, (plane, plane, fringe), total * Y
    )
    up, h_out, h_in = exchange(start, up)
    *first, f_up = kernel_call(
        functools.partial(first_kernel, X),
        "first",
        (*start, *slopes(start), h_out, h_in, up, lam, *drags),
        (plane, plane, fringe),
        100 * total * Y,
    )
    up, h_out, h_in = exchange(first, f_up)
    rate = slopes(first)
    done = {}
    for side, halo in ((1, h_in), (0, h_out)):
        parts = kernel_call(
            functools.partial(last_kernel, X, side),
            f"last{side}",
            (start[side], *first, rate[side], halo, up, lam, *drags),
            [((3, X, Y), f32)] * 4,
            60 * total * Y,
        )
        for b in range(4):
            done[b, side] = swap(parts[b], b) if b else parts[0]
    pieces = [done[b, side] for b in range(4) for side in range(2)]
    advanced = pl.pallas_call(
        functools.partial(unpack_kernel, X, L),
        grid=(Y // lanes,),
        in_specs=[pl.BlockSpec(memory_space=pltpu.VMEM)] * 8,
        out_specs=pl.BlockSpec((3 * X * L, lanes), lambda i: (0, i)),
        out_shape=jax.ShapeDtypeStruct((3 * X * L, Y), f32),
        compiler_params=pltpu.CompilerParams(vmem_limit_bytes=24 << 20),
        name="unpack",
    )(*[pltpu.with_memory_space_constraint(x, pltpu.VMEM) for x in pieces])
    return advanced.reshape(velocity.shape)


def shards(velocity, drag, stream_gain, span_gain):
    groups = lax.axis_size("gx")
    levels, width = velocity.shape[3:]
    fits = groups == 4 and levels == 2 * groups and width % lanes == 0
    form = transposed_step if fits else general_step
    return form(velocity, drag, stream_gain, span_gain)


def solution(mesh):
    placed = (P("sec", None, "gx", "gz", None), P("sec", "gx", "gz", None), P(), P())
    return jax.shard_map(
        shards,
        mesh=mesh,
        in_specs=placed,
        out_specs=P("sec", None, "gx", "gz", None),
        check_vma=False,
    )
```
